512 devices in a mesh: section: 16 (over x_lo, z), dp: 32 (over x_hi, y, core).
Axes of the slice: x: 4 (x_hi: 2, x_lo: 2; x = x_hi * 2 + x_lo), y: 8, z: 8, core: 2. Of those that a mesh axis runs over, the one named last changes fastest.
Arguments:
- acts_down: bfloat16 [3, 16, 32, 16, 16, 256], P(None, 'section', 'dp'), may hold values from -6 to 6
- acts_up: bfloat16 [3, 16, 32, 16, 16, 256], P(None, 'section', 'dp'), may hold values from -6 to 6
- front_down: bfloat16 [16, 32, 16, 16, 256], P('section', 'dp'), may hold values from -6 to 6
- front_up: bfloat16 [16, 32, 16, 16, 256], P('section', 'dp'), may hold values from -6 to 6
- master: float32 [16, 2304, 256], P('section', 'dp'), may hold values from -4 to 4
- moment_first: float32 [16, 2304, 256], P('section', 'dp'), may hold values from -36 to 36
- moment_second: float32 [16, 2304, 256], P('section', 'dp'), may hold values from 10 to 100
Outputs:
- dx_down: bfloat16 [3, 16, 32, 16, 16, 256], P(None, 'section', 'dp')
- dx_up: bfloat16 [3, 16, 32, 16, 16, 256], P(None, 'section', 'dp')
- new_weight: bfloat16 [16, 2304, 256], P('section', 'dp')
- new_master: float32 [16, 2304, 256], P('section', 'dp')
- new_first: float32 [16, 2304, 256], P('section', 'dp')
- new_second: float32 [16, 2304, 256], P('section', 'dp')
The draws below stay inside these ranges and needn't reach their ends.
All inputs are finite; a program needn't handle non-finite values.
Results may differ from the reference program's by a relative error of at most 0.0025.
The reference program's roundings to bfloat16 on the way (of `weight` and `hidden`) count: a program that leaves them out, or rounds other values in their place, can miss the bound.
Values may be sent and summed in bfloat16 or wider, within the bound.
No kernel may reach another device: no remote copies, remote signals or barrier semaphores. Data moves between devices by JAX's collectives and lax.ppermute only.
A program may use at most 64 MiB of HBM per device.

```python
import math
import jax
import jax.numpy as jnp
from jax import lax

C = 256
HH = 16
WW = 16
TICKS = 3
SECTIONS = 16
IMAGES = 32
N_DP = 32


def shard_levels(stream_key, dims, cuts, least, high):
    def one(axis_at, parts):
        draws = jax.random.uniform(jax.random.fold_in(jax.random.fold_in(stream_key, 6), axis_at), (parts,), jnp.float32, least / len(cuts), high / len(cuts))
        return jnp.repeat(jnp.exp(draws), dims[axis_at] // parts).reshape((-1,) + (1,) * (len(dims) - axis_at - 1))

    factor_of = one(*cuts[0])
    for cut in cuts[1:]:
        factor_of = factor_of * one(*cut)
    return factor_of


def bell_draw(own_key, extent, scale, reach, cuts=(), held_as=jnp.bfloat16):
    result = scale * jax.random.normal(own_key, extent, jnp.float32)
    if cuts:
        result = result * shard_levels(own_key, extent, cuts, -0.22, 0.18)
    return jnp.clip(result, -reach, reach).astype(held_as)


def setup_inputs(seed: int = 0) -> dict:
    arg_keys = jax.random.split(jax.random.key(seed), 8)
    return {
        "acts_down": bell_draw(arg_keys[0], (TICKS, SECTIONS, IMAGES, HH, WW, C), 1.0, 6.0, ((1, 16), (2, 32))),
        "acts_up": bell_draw(arg_keys[1], (TICKS, SECTIONS, IMAGES, HH, WW, C), 1.0, 6.0, ((1, 16), (2, 32))),
        "front_down": bell_draw(arg_keys[2], (SECTIONS, IMAGES, HH, WW, C), 1.0, 6.0, ((0, 16), (1, 32))),
        "front_up": bell_draw(arg_keys[3], (SECTIONS, IMAGES, HH, WW, C), 1.0, 6.0, ((0, 16), (1, 32))),
        "master": bell_draw(arg_keys[4], (SECTIONS, 9 * C, C), 1.0, 4.0, ((0, 16), (1, 32)), jnp.float32),
        "moment_first": bell_draw(arg_keys[5], (SECTIONS, 9 * C, C), 6.0, 36.0, ((0, 16), (1, 32)), jnp.float32),
        "moment_second": jnp.clip(jnp.exp(math.log(100.0) - 2.3025851 * jax.random.uniform(arg_keys[6], (SECTIONS, 9 * C, C), jnp.float32) ** shard_levels(arg_keys[6], (SECTIONS, 9 * C, C), ((0, 16), (1, 32)), -0.2, 0.2)), 10.0, 100.0),
    }


beta_first = 0.9
beta_second = 0.95
learn_rate = 0.01
decay_rate = 0.1
epsilon = 1e-08

def shifted_taps(feature, direction):
    images, height, columns, channels = feature.shape
    padded = jnp.pad(feature, ((0, 0), (1, 1), (1, 1), (0, 0)))
    pieces = []
    for row_step in range(3):
        for col_step in range(3):
            row_start = 1 + direction * (row_step - 1)
            col_start = 1 + direction * (col_step - 1)
            pieces.append(padded[:, row_start:row_start + height, col_start:col_start + columns, :])
    return jnp.concatenate(pieces, axis=3).reshape(images * height * columns, 9 * channels)

def section_front(inputs, incoming, weight):
    channels = inputs.shape[-1]
    factor = (9 * channels) ** (-0.5)
    taps_front = shifted_taps(incoming, -1).reshape(-1, 9, channels).astype(jnp.float32)
    kernel = weight.reshape(9, channels, channels).astype(jnp.float32)
    grad_hidden = lax.dot_general(taps_front, kernel, (((1, 2), (0, 2)), ((), ())), preferred_element_type=jnp.float32)
    grad_hidden = factor * grad_hidden.reshape(inputs.shape)
    widened = inputs.astype(jnp.float32)
    _, pullback = jax.vjp(jax.nn.gelu, widened)
    return (incoming.astype(jnp.float32) + pullback(grad_hidden)[0]).astype(jnp.bfloat16)

def weight_grad(inputs, seen):
    channels = inputs.shape[-1]
    factor = (9 * channels) ** (-0.5)
    summed = jnp.zeros((N_DP, 9 * channels, channels), jnp.float32)
    for tick_index in range(TICKS):
        hidden = jax.nn.gelu(inputs[tick_index].astype(jnp.float32)).astype(jnp.bfloat16)
        taps_hidden = shifted_taps(hidden, 1).reshape(N_DP, -1, 9 * channels).astype(jnp.float32)
        fronts = seen[tick_index].reshape(N_DP, -1, channels).astype(jnp.float32)
        summed = summed + jnp.einsum('gpk,gpc->gkc', taps_hidden, fronts)
    partial_value = (factor * summed).astype(jnp.bfloat16)
    partial_value = lax.optimization_barrier(partial_value)
    return lax.optimization_barrier(jnp.sum(partial_value.astype(jnp.float32), axis=0))

def reference(acts_down, acts_up, front_down, front_up, master, moment_first, moment_second):
    weight = master.astype(jnp.bfloat16)
    mirror = weight[::-1]
    grad_down = front_down
    grad_up = front_up
    seen_down = []
    seen_up = []
    outs_down = []
    outs_up = []
    for tick_index in range(TICKS):
        seen_down.append(grad_down)
        seen_up.append(grad_up)
        next_down = lax.map(lambda members: section_front(*members), (acts_down[tick_index], grad_down, weight))
        next_up = lax.map(lambda members: section_front(*members), (acts_up[tick_index], grad_up, mirror))
        outs_down.append(next_down)
        outs_up.append(next_up)
        zeros_row = jnp.zeros_like(next_down[:1])
        grad_down = jnp.concatenate([next_down[1:], zeros_row], axis=0)
        grad_up = jnp.concatenate([zeros_row, next_up[:-1]], axis=0)
    stack_down = jnp.stack(seen_down, axis=1)
    stack_up = jnp.stack(seen_up, axis=1)
    sum_down = lax.map(lambda members: weight_grad(*members), (jnp.swapaxes(acts_down, 0, 1), stack_down))
    sum_up = lax.map(lambda members: weight_grad(*members), (jnp.swapaxes(acts_up, 0, 1), stack_up))
    gradient = sum_down + sum_up[::-1]
    new_first = beta_first * moment_first + (1.0 - beta_first) * gradient
    new_second = beta_second * moment_second + (1.0 - beta_second) * gradient * gradient
    new_master = master - learn_rate * (new_first / (jnp.sqrt(new_second) + epsilon) + decay_rate * master)
    return (jnp.stack(outs_down), jnp.stack(outs_up), new_master.astype(jnp.bfloat16), new_master, new_first, new_second)
```

```python
import functools
import jax
import jax.numpy as jnp
from jax import lax
from jax.experimental import pallas as pl
from jax.experimental.pallas import tpu as pltpu
from jax.sharding import Mesh, PartitionSpec as P


def gelu_kernel(act_ref, hid_ref, slope_ref):
    x = act_ref[0].astype(jnp.float32)
    cube = 0.044715 * x * x * x
    t = jnp.tanh(0.7978845608028654 * (x + cube))
    half = 0.5 * (1.0 + t)
    hidden = (x * half).astype(jnp.bfloat16)
    hid_ref[0] = hidden.astype(jnp.float32).T.astype(jnp.bfloat16)
    inner = 0.7978845608028654 * (1.0 + 3.0 * 0.044715 * x * x)
    slope_ref[0] = half + 0.5 * x * (1.0 - t * t) * inner


def gelu_parts(acts):
    n, pixels, channels = acts.shape
    return pl.pallas_call(
        gelu_kernel,
        grid=(n,),
        in_specs=[pl.BlockSpec((1, pixels, channels), lambda i: (i, 0, 0))],
        out_specs=[
            pl.BlockSpec((1, channels, pixels), lambda i: (i, 0, 0)),
            pl.BlockSpec((1, pixels, channels), lambda i: (i, 0, 0)),
        ],
        out_shape=[
            jax.ShapeDtypeStruct((n, channels, pixels), jnp.bfloat16),
            jax.ShapeDtypeStruct((n, pixels, channels), jnp.float32),
        ],
        name="gelu_parts",
    )(acts)


def fill_taps(front, pad_ref, width):
    pixels = front.shape[0]
    wide = front.astype(jnp.float32)
    column = lax.broadcasted_iota(jnp.int32, wide.shape, 0) % width
    after = jnp.where(column == width - 1, 0.0, pltpu.roll(wide, pixels - 1, 0))
    before = jnp.where(column == 0, 0.0, pltpu.roll(wide, 1, 0))
    empty = jnp.zeros((width, front.shape[1]), jnp.bfloat16)
    for b, piece in enumerate((after.astype(jnp.bfloat16), front, before.astype(jnp.bfloat16))):
        pad_ref[b, 0:width] = empty
        pad_ref[b, width : width + pixels] = piece
        pad_ref[b, width + pixels : 2 * width + pixels] = empty


def tick_kernel(width, factor, front_ref, weight_ref, slope_ref, out_ref, pad_ref):
    front = front_ref[0]
    pixels, channels = front.shape
    fill_taps(front, pad_ref, width)
    total = jnp.zeros((pixels, channels), jnp.float32)
    for a in range(3):
        for b in range(3):
            row = (3 * a + b) * channels
            total += lax.dot_general(
                pad_ref[b, (2 - a) * width : (2 - a) * width + pixels],
                weight_ref[0, row : row + channels],
                (((1,), (1,)), ((), ())),
                preferred_element_type=jnp.float32,
            )
    out_ref[0] = (front.astype(jnp.float32) + slope_ref[0] * (factor * total)).astype(jnp.bfloat16)


def tick(fronts, weights, slopes, width):
    n, pixels, channels = fronts.shape
    factor = (9 * channels) ** -0.5
    whole = lambda i: (i, 0, 0)
    shared = weights.shape[0] == 1
    return pl.pallas_call(
        functools.partial(tick_kernel, width, factor),
        grid=(n,),
        in_specs=[
            pl.BlockSpec((1, pixels, channels), whole),
            pl.BlockSpec((1, 9 * channels, channels), (lambda i: (0, 0, 0)) if shared else whole),
            pl.BlockSpec((1, pixels, channels), whole),
        ],
        out_specs=pl.BlockSpec((1, pixels, channels), whole),
        out_shape=jax.ShapeDtypeStruct(fronts.shape, jnp.bfloat16),
        scratch_shapes=[pltpu.VMEM((3, pixels + 2 * width, channels), jnp.bfloat16)],
        name="tick",
    )(fronts, weights, slopes)


def term_kernel(parts, ticks, width, factor, *refs):
    hid_refs, front_refs, out_ref, pad_ref = refs[:parts], refs[parts:-2], refs[-2], refs[-1]
    for t, front_ref in enumerate(front_refs):
        fill_taps(front_ref[0], pad_ref.at[t], width)
    hiddens = [ref.at[t] for ref in hid_refs for t in range(ref.shape[0])]
    channels, pixels = hiddens[0].shape
    for a in range(3):
        for b in range(3):
            row = (3 * a + b) * channels
            total = jnp.zeros((channels, channels), jnp.float32)
            for t, hidden in enumerate(hiddens):
                total += lax.dot_general(
                    hidden[...],
                    pad_ref[t, b, (2 - a) * width : (2 - a) * width + pixels],
                    (((1,), (0,)), ((), ())),
                    preferred_element_type=jnp.float32,
                )
            out_ref[row : row + channels] = (factor * total).astype(jnp.bfloat16)


def weight_term(hiddens, fronts, width):
    channels, pixels = hiddens[0].shape[1:]
    factor = (9 * channels) ** -0.5
    return pl.pallas_call(
        functools.partial(term_kernel, len(hiddens), len(fronts), width, factor),
        out_shape=jax.ShapeDtypeStruct((9 * channels, channels), jnp.bfloat16),
        scratch_shapes=[
            pltpu.VMEM((len(fronts), 3, pixels + 2 * width, channels), jnp.bfloat16)
        ],
        name="weight_term",
    )(*hiddens, *fronts)


beta_first = 0.9
beta_second = 0.95
learn_rate = 0.01
decay_rate = 0.1
epsilon = 1e-08

SECTION = ("x_lo", "z")
CHIPS = ("x_hi", "y")


def to_mirror(value):
    length = lax.axis_size(SECTION)
    return lax.ppermute(value, SECTION, [(i, length - 1 - i) for i in range(length)])


def from_next(value):
    length = lax.axis_size(SECTION)
    return lax.ppermute(value, SECTION, [(i + 1, i) for i in range(length - 1)])


def to_partner(value):
    return lax.ppermute(value, "core", [(0, 1), (1, 0)])


def gather_rows(rows):
    chips = lax.axis_size(CHIPS)
    spread = jnp.broadcast_to(rows[None], (chips, *rows.shape))
    mine = lax.all_to_all(spread, CHIPS, 0, 0, tiled=True)
    other = to_partner(mine)
    first = lax.axis_index("core") == 0
    whole = jnp.stack([jnp.where(first, mine, other), jnp.where(first, other, mine)], axis=1)
    return whole.reshape(-1, rows.shape[1])


def scatter_sum(part):
    chips = lax.axis_size(CHIPS)
    core = lax.axis_index("core")
    split = part.reshape(chips, 2, -1, part.shape[1])
    given = lax.dynamic_index_in_dim(split, 1 - core, 1, keepdims=False)
    kept = lax.dynamic_index_in_dim(split, core, 1, keepdims=False)
    pair = (kept.astype(jnp.float32) + to_partner(given).astype(jnp.float32)).astype(jnp.bfloat16)
    pieces = lax.all_to_all(pair, CHIPS, 0, 0, tiled=True)
    return jnp.sum(pieces.astype(jnp.float32), axis=0)


def per_device(acts_down, acts_up, front_down, front_up, master, moment_first, moment_second):
    ticks, _, _, height, width, channels = acts_down.shape
    pixels = height * width
    flat = (1, pixels, channels)
    front_down = front_down.reshape(flat)
    front_up = to_mirror(front_up.reshape(flat))
    far_acts = [to_mirror(acts_up[t].reshape(flat)) for t in range(ticks)]
    weight = gather_rows(master[0].astype(jnp.bfloat16))[None]
    hid_down, slope_down = gelu_parts(acts_down.reshape(ticks, pixels, channels))
    hid_up, slope_up = [], []
    for t in range(ticks):
        hidden, slope = gelu_parts(far_acts[t])
        hid_up.append(hidden)
        slope_up.append(slope)
    seen_down, seen_up = [front_down], [front_up]
    outs_down, outs_up = [], []
    for t in range(ticks):
        next_down = tick(seen_down[t], weight, slope_down[t : t + 1], width)
        next_up = tick(seen_up[t], weight, slope_up[t], width)
        outs_down.append(next_down)
        outs_up.append(to_mirror(next_up))
        if t + 1 < ticks:
            seen_down.append(from_next(next_down))
            seen_up.append(from_next(next_up))
    part = weight_term([hid_down, *hid_up], seen_down + seen_up, width)
    gradient = scatter_sum(part)
    old_master = master[0]
    new_first = beta_first * moment_first[0] + (1.0 - beta_first) * gradient
    new_second = beta_second * moment_second[0] + (1.0 - beta_second) * gradient * gradient
    new_master = old_master - learn_rate * (
        new_first / (jnp.sqrt(new_second) + epsilon) + decay_rate * old_master
    )
    shape = (ticks, 1, 1, height, width, channels)
    return (
        jnp.concatenate(outs_down).reshape(shape),
        jnp.concatenate(outs_up).reshape(shape),
        new_master.astype(jnp.bfloat16)[None],
        new_master[None],
        new_first[None],
        new_second[None],
    )


def solution(mesh):
    fine = Mesh(
        mesh.devices.reshape(2, 8, 2, 8, 2), ("x_lo", "z", "x_hi", "y", "core")
    )
    dp = (*CHIPS, "core")
    images = P(None, SECTION, dp, None, None, None)
    fronts = P(SECTION, dp, None, None, None)
    rows = P(SECTION, dp, None)
    return jax.shard_map(
        per_device,
        mesh=fine,
        in_specs=(images, images, fronts, fronts, rows, rows, rows),
        out_specs=(images, images, rows, rows, rows, rows),
        check_vma=False,
    )
```

```python
import functools
import jax
import jax.numpy as jnp
from jax import lax
from jax.experimental import pallas as pl
from jax.experimental.pallas import tpu as pltpu
from jax.sharding import Mesh, PartitionSpec as P


VMEM = pl.BlockSpec(memory_space=pltpu.VMEM)
SMEM = pl.BlockSpec(memory_space=pltpu.SMEM)


def on_chip(value):
    return pltpu.with_memory_space_constraint(value, pltpu.VMEM)


def call(body, outs, args, scratch=(), scalars=0, alias=None):
    specs = [SMEM] * scalars + [VMEM] * (len(args) - scalars)
    args = [*args[:scalars], *map(on_chip, args[scalars:])]
    return pl.pallas_call(
        body,
        in_specs=specs,
        out_specs=[VMEM] * len(outs),
        out_shape=[pltpu.VMEM(shape, dtype) for shape, dtype in outs],
        scratch_shapes=list(scratch),
        input_output_aliases=alias or {},
        compiler_params=pltpu.CompilerParams(vmem_limit_bytes=16 << 20),
    )(*args)


def gelu_kernel(act_ref, hid_ref, slope_ref):
    for t in range(act_ref.shape[0]):
        x = act_ref[t].astype(jnp.float32)
        cube = 0.044715 * x * x * x
        bent = jnp.tanh(0.7978845608028654 * (x + cube))
        half = 0.5 * (1.0 + bent)
        hidden = (x * half).astype(jnp.bfloat16)
        hid_ref[t] = hidden.astype(jnp.float32).T.astype(jnp.bfloat16)
        inner = 0.7978845608028654 * (1.0 + 3.0 * 0.044715 * x * x)
        slope_ref[t] = half + 0.5 * x * (1.0 - bent * bent) * inner


def gelu_parts(acts):
    n, pixels, channels = acts.shape
    outs = [((n, channels, pixels), jnp.bfloat16), ((n, pixels, channels), jnp.float32)]
    return call(gelu_kernel, outs, [acts])


def fill_taps(front, pad_ref, width):
    pixels = front.shape[0]
    wide = front.astype(jnp.float32)
    column = lax.broadcasted_iota(jnp.int32, wide.shape, 0) % width
    after = jnp.where(column == width - 1, 0.0, pltpu.roll(wide, pixels - 1, 0))
    before = jnp.where(column == 0, 0.0, pltpu.roll(wide, 1, 0))
    empty = jnp.zeros((width, front.shape[1]), jnp.bfloat16)
    for b, piece in enumerate((after.astype(jnp.bfloat16), front, before.astype(jnp.bfloat16))):
        pad_ref[b, 0:width] = empty
        pad_ref[b, width : width + pixels] = piece
        pad_ref[b, width + pixels : 2 * width + pixels] = empty


def pads(count, pixels, width, channels):
    return pltpu.VMEM((count, 3, pixels + 2 * width, channels), jnp.bfloat16)


def tick_kernel(t, width, factor, front_ref, weight_ref, slope_ref, *refs):
    earlier, (out_ref, *pair, pad_ref) = refs[: len(refs) // 2 - 1], refs[len(refs) // 2 - 1 :]
    front = front_ref[...]
    pixels, channels = front.shape
    fill_taps(front, pad_ref.at[0], width)
    total = jnp.zeros((pixels, channels), jnp.float32)
    for a in range(3):
        for b in range(3):
            row = (3 * a + b) * channels
            total += lax.dot_general(
                pad_ref[0, b, (2 - a) * width : (2 - a) * width + pixels],
                weight_ref[row : row + channels],
                (((1,), (1,)), ((), ())),
                preferred_element_type=jnp.float32,
            )
    out = (front.astype(jnp.float32) + slope_ref[t] * (factor * total)).astype(jnp.bfloat16)
    out_ref[...] = out
    if pair:
        pair[0][0] = earlier[0][...]
        pair[0][1] = out


def tick(front, weight, slopes, t, width, earlier=None):
    pixels, channels = front.shape
    factor = (9 * channels) ** -0.5
    outs = [(front.shape, jnp.bfloat16)]
    args = [front, weight, slopes]
    if earlier is not None:
        outs.append(((2, *front.shape), jnp.bfloat16))
        args.append(earlier)
    return call(
        functools.partial(tick_kernel, t, width, factor),
        outs,
        args,
        [pads(1, pixels, width, channels)],
    )


def add_terms(hiddens, front_refs, pad_ref, width, write):
    for j, front_ref in enumerate(front_refs):
        fill_taps(front_ref[...], pad_ref.at[j], width)
    channels, pixels = hiddens[0].shape
    for a in range(3):
        for b in range(3):
            total = jnp.zeros((channels, channels), jnp.float32)
            for j, hidden in enumerate(hiddens):
                total += lax.dot_general(
                    hidden[...],
                    pad_ref[j, b, (2 - a) * width : (2 - a) * width + pixels],
                    (((1,), (0,)), ((), ())),
                    preferred_element_type=jnp.float32,
                )
            write((3 * a + b) * channels, total)


def early_kernel(ticks, width, hid_down_ref, hid_up_ref, *refs):
    front_refs, (out_ref, pad_ref) = refs[:-2], refs[-2:]
    hiddens = [hid_down_ref.at[t] for t in ticks] + [hid_up_ref.at[t] for t in ticks]

    def write(row, total):
        out_ref[row : row + total.shape[0]] = total

    add_terms(hiddens, front_refs, pad_ref, width, write)


def early_terms(hid_down, hid_up, fronts, ticks, width):
    channels, pixels = hid_down.shape[1:]
    return call(
        functools.partial(early_kernel, ticks, width),
        [((9 * channels, channels), jnp.float32)],
        [hid_down, hid_up, *fronts],
        [pads(len(fronts), pixels, width, channels)],
    )[0]


def last_kernel(t, width, factor, core_ref, hid_down_ref, hid_up_ref, total_ref, *refs):
    front_refs, (kept_ref, given_ref, sum_ref, pad_ref) = refs[:-4], refs[-4:]
    rows = kept_ref.shape[1]

    def write(row, total):
        at = slice(row, row + total.shape[0])
        sum_ref[at] = factor * (total_ref[at] + total)

    add_terms([hid_down_ref.at[t], hid_up_ref.at[t]], front_refs, pad_ref, width, write)
    for core, places in enumerate(((kept_ref, given_ref), (given_ref, kept_ref))):

        @pl.when(core_ref[0] == core)
        def _():
            for i in range(2 * kept_ref.shape[0]):
                places[i % 2][i // 2] = sum_ref[i * rows : (i + 1) * rows].astype(jnp.bfloat16)


def last_terms(core, hid_down, hid_up, total, fronts, t, chips, width):
    channels, pixels = hid_down.shape[1:]
    half = (chips, 9 * channels // (2 * chips), channels)
    return call(
        functools.partial(last_kernel, t, width, (9 * channels) ** -0.5),
        [(half, jnp.bfloat16), (half, jnp.bfloat16)],
        [core, hid_down, hid_up, total, *fronts],
        [pltpu.VMEM((9 * channels, channels), jnp.float32), pads(len(fronts), pixels, width, channels)],
        scalars=1,
    )


def weave_kernel(core_ref, mine_ref, other_ref, out_ref):
    core = core_ref[0]
    for i in range(mine_ref.shape[0]):
        out_ref[i, core] = mine_ref[i]
        out_ref[i, 1 - core] = other_ref[i]


def weave(core, mine, other):
    chips, rows, channels = mine.shape
    whole = call(
        weave_kernel, [((chips, 2, rows, channels), jnp.bfloat16)], [core, mine, other], scalars=1
    )[0]
    return whole.reshape(-1, channels)


beta_first = 0.9
beta_second = 0.95
learn_rate = 0.01
decay_rate = 0.1
epsilon = 1e-08

SECTION = ("x_lo", "z")
CHIPS = ("x_hi", "y")


def to_mirror(value):
    length = lax.axis_size(SECTION)
    return lax.ppermute(value, SECTION, [(i, length - 1 - i) for i in range(length)])


def from_next(value):
    length = lax.axis_size(SECTION)
    return lax.ppermute(value, SECTION, [(i + 1, i) for i in range(length - 1)])


def to_partner(value):
    return lax.ppermute(value, "core", [(0, 1), (1, 0)])


def step(acts_down, acts_up, front_down, front_up, master, moment_first, moment_second):
    ticks, _, _, height, width, channels = acts_down.shape
    flat = (height * width, channels)
    chips = lax.axis_size(CHIPS)
    core = lax.axis_index("core").astype(jnp.int32).reshape(1)
    front_up = to_mirror(front_up.reshape(flat))
    acts_up = to_mirror(acts_up.reshape(ticks, *flat))
    rows = master[0].astype(jnp.bfloat16)
    mine = lax.all_to_all(jnp.broadcast_to(rows[None], (chips, *rows.shape)), CHIPS, 0, 0, tiled=True)
    hid_down, slope_down = gelu_parts(acts_down.reshape(ticks, *flat))
    hid_up, slope_up = gelu_parts(acts_up)
    other = to_partner(mine)
    weight = weave(core, mine, other)
    down, up = [front_down.reshape(flat)], [front_up]
    outs_down, outs_up = [], []
    for t in range(ticks):
        next_down = tick(down[t], weight, slope_down, t, width)[0]
        if t == 1:
            next_up, pair = tick(up[t], weight, slope_up, t, width, outs_up[0])
        else:
            next_up = tick(up[t], weight, slope_up, t, width)[0]
        outs_down.append(next_down)
        outs_up.append(next_up)
        if t + 1 < ticks:
            down.append(from_next(next_down))
            up.append(from_next(next_up))
    total = early_terms(hid_down, hid_up, down[:2] + up[:2], (0, 1), width)
    pair = to_mirror(pair)
    kept, given = last_terms(core, hid_down, hid_up, total, [down[2], up[2]], 2, chips, width)
    taken = to_partner(given)
    both = (kept.astype(jnp.float32) + taken.astype(jnp.float32)).astype(jnp.bfloat16)
    pieces = lax.all_to_all(both, CHIPS, 0, 0, tiled=True)
    last = to_mirror(outs_up[2])
    gradient = jnp.sum(pieces.astype(jnp.float32), axis=0)
    old_master = master[0]
    new_first = beta_first * moment_first[0] + (1.0 - beta_first) * gradient
    new_second = beta_second * moment_second[0] + (1.0 - beta_second) * gradient * gradient
    new_master = old_master - learn_rate * (
        new_first / (jnp.sqrt(new_second) + epsilon) + decay_rate * old_master
    )
    shape = (ticks, 1, 1, height, width, channels)
    return (
        jnp.stack(outs_down).reshape(shape),
        jnp.concatenate([pair, last[None]]).reshape(shape),
        new_master.astype(jnp.bfloat16)[None],
        new_master[None],
        new_first[None],
        new_second[None],
    )


def solution(mesh):
    fine = Mesh(
        mesh.devices.reshape(2, 8, 2, 8, 2), ("x_lo", "z", "x_hi", "y", "core")
    )
    dp = (*CHIPS, "core")
    images = P(None, SECTION, dp, None, None, None)
    fronts = P(SECTION, dp, None, None, None)
    rows = P(SECTION, dp, None)
    return jax.shard_map(
        step,
        mesh=fine,
        in_specs=(images, images, fronts, fronts, rows, rows, rows),
        out_specs=(images, images, rows, rows, rows, rows),
        check_vma=False,
    )
```

```python
import functools
import jax
import jax.numpy as jnp
from jax import lax
from jax.experimental import pallas as pl
from jax.experimental.pallas import tpu as pltpu
from jax.sharding import Mesh, PartitionSpec as P


VMEM = pl.BlockSpec(memory_space=pltpu.VMEM)
SMEM = pl.BlockSpec(memory_space=pltpu.SMEM)


def on_chip(value):
    return pltpu.with_memory_space_constraint(value, pltpu.VMEM)


def call(body, outs, args, scratch=(), scalars=0, off_chip=False):
    specs = [SMEM] * scalars + [VMEM] * (len(args) - scalars)
    args = [*args[:scalars], *map(on_chip, args[scalars:])]
    return pl.pallas_call(
        body,
        in_specs=specs,
        out_specs=[VMEM] * len(outs),
        out_shape=[(jax.ShapeDtypeStruct if off_chip else pltpu.VMEM)(*out) for out in outs],
        scratch_shapes=list(scratch),
        compiler_params=pltpu.CompilerParams(vmem_limit_bytes=16 << 20),
    )(*args)


def spread_kernel(rows_ref, out_ref):
    rows = rows_ref[...].astype(jnp.bfloat16)
    for i in range(out_ref.shape[0]):
        out_ref[i] = rows


def spread(rows, count):
    return call(spread_kernel, [((count, *rows.shape), jnp.bfloat16)], [rows])[0]


def add_kernel(one_ref, two_ref, out_ref):
    total = one_ref[...].astype(jnp.float32) + two_ref[...].astype(jnp.float32)
    out_ref[...] = total.astype(jnp.bfloat16)


def pair_add(one, two):
    return call(add_kernel, [(one.shape, jnp.bfloat16)], [one, two])[0]


def bend(x):
    bent = jnp.tanh(0.7978845608028654 * (x + 0.044715 * x * x * x))
    return bent, 0.5 * (1.0 + bent)


def hidden_kernel(*refs):
    acts, outs = refs[: len(refs) // 2], refs[len(refs) // 2 :]
    for act_ref, out_ref in zip(acts, outs):
        x = act_ref[...].astype(jnp.float32)
        hidden = (x * bend(x)[1]).astype(jnp.bfloat16)
        out_ref[...] = hidden.astype(jnp.float32).T.astype(jnp.bfloat16)


def hidden_parts(acts):
    outs = [(act.shape[::-1], jnp.bfloat16) for act in acts]
    return call(hidden_kernel, outs, acts, off_chip=True)


def fill_taps(front, pad_ref, width):
    pixels = front.shape[0]
    wide = front.astype(jnp.float32)
    column = lax.broadcasted_iota(jnp.int32, wide.shape, 0) % width
    after = jnp.where(column == width - 1, 0.0, pltpu.roll(wide, pixels - 1, 0))
    before = jnp.where(column == 0, 0.0, pltpu.roll(wide, 1, 0))
    empty = jnp.zeros((width, front.shape[1]), jnp.bfloat16)
    for b, piece in enumerate((after.astype(jnp.bfloat16), front, before.astype(jnp.bfloat16))):
        pad_ref[b, 0:width] = empty
        pad_ref[b, width : width + pixels] = piece
        pad_ref[b, width + pixels : 2 * width + pixels] = empty


def pads(count, pixels, width, channels):
    return pltpu.VMEM((count, 3, pixels + 2 * width, channels), jnp.bfloat16)


def tick_kernel(width, factor, front_ref, weight_ref, act_ref, *refs):
    earlier, (out_ref, *pair, pad_ref) = refs[: len(refs) // 2 - 1], refs[len(refs) // 2 - 1 :]
    front = front_ref[...]
    pixels, channels = front.shape
    fill_taps(front, pad_ref.at[0], width)
    total = jnp.zeros((pixels, channels), jnp.float32)
    for a in range(3):
        for b in range(3):
            row = (3 * a + b) * channels
            total += lax.dot_general(
                pad_ref[0, b, (2 - a) * width : (2 - a) * width + pixels],
                weight_ref[row : row + channels],
                (((1,), (1,)), ((), ())),
                preferred_element_type=jnp.float32,
            )
    x = act_ref[...].astype(jnp.float32)
    bent, half = bend(x)
    inner = 0.7978845608028654 * (1.0 + 3.0 * 0.044715 * x * x)
    slope = half + 0.5 * x * (1.0 - bent * bent) * inner
    out = (front.astype(jnp.float32) + slope * (factor * total)).astype(jnp.bfloat16)
    out_ref[...] = out
    if pair:
        pair[0][0] = earlier[0][...]
        pair[0][1] = out


def tick(front, weight, act, width, earlier=None):
    pixels, channels = front.shape
    factor = (9 * channels) ** -0.5
    outs = [(front.shape, jnp.bfloat16)]
    args = [front, weight, act]
    if earlier is not None:
        outs.append(((2, *front.shape), jnp.bfloat16))
        args.append(earlier)
    return call(
        functools.partial(tick_kernel, width, factor),
        outs,
        args,
        [pads(1, pixels, width, channels)],
    )


def add_terms(hiddens, front_refs, pad_ref, width, write):
    for j, front_ref in enumerate(front_refs):
        fill_taps(front_ref[...], pad_ref.at[j], width)
    channels, pixels = hiddens[0].shape
    for a in range(3):
        for b in range(3):
            total = jnp.zeros((channels, channels), jnp.float32)
            for j, hidden in enumerate(hiddens):
                total += lax.dot_general(
                    hidden[...],
                    pad_ref[j, b, (2 - a) * width : (2 - a) * width + pixels],
                    (((1,), (0,)), ((), ())),
                    preferred_element_type=jnp.float32,
                )
            write((3 * a + b) * channels, total)


def early_kernel(width, *refs):
    count = len(refs) // 2 - 1
    hid_refs, front_refs, (out_ref, pad_ref) = refs[:count], refs[count:-2], refs[-2:]

    def write(row, total):
        out_ref[row : row + total.shape[0]] = total

    add_terms(hid_refs, front_refs, pad_ref, width, write)


def early_terms(hiddens, fronts, width):
    channels, pixels = hiddens[0].shape
    return call(
        functools.partial(early_kernel, width),
        [((9 * channels, channels), jnp.float32)],
        [*hiddens, *fronts],
        [pads(len(fronts), pixels, width, channels)],
    )[0]


def last_kernel(width, factor, core_ref, total_ref, *refs):
    count = len(refs) // 2 - 2
    hid_refs, front_refs = refs[:count], refs[count:-4]
    kept_ref, given_ref, sum_ref, pad_ref = refs[-4:]
    rows = kept_ref.shape[1]

    def write(row, total):
        at = slice(row, row + total.shape[0])
        sum_ref[at] = factor * (total_ref[at] + total)

    add_terms(hid_refs, front_refs, pad_ref, width, write)
    for core, places in enumerate(((kept_ref, given_ref), (given_ref, kept_ref))):

        @pl.when(core_ref[0] == core)
        def _():
            for i in range(2 * kept_ref.shape[0]):
                places[i % 2][i // 2] = sum_ref[i * rows : (i + 1) * rows].astype(jnp.bfloat16)


def last_terms(core, total, hiddens, fronts, chips, width):
    channels, pixels = hiddens[0].shape
    half = (chips, 9 * channels // (2 * chips), channels)
    return call(
        functools.partial(last_kernel, width, (9 * channels) ** -0.5),
        [(half, jnp.bfloat16), (half, jnp.bfloat16)],
        [core, total, *hiddens, *fronts],
        [
            pltpu.VMEM((9 * channels, channels), jnp.float32),
            pads(len(fronts), pixels, width, channels),
        ],
        scalars=1,
    )


def weave_kernel(core_ref, mine_ref, other_ref, out_ref):
    core = core_ref[0]
    for i in range(mine_ref.shape[0]):
        out_ref[i, core] = mine_ref[i]
        out_ref[i, 1 - core] = other_ref[i]


def weave(core, mine, other):
    chips, rows, channels = mine.shape
    whole = call(
        weave_kernel, [((chips, 2, rows, channels), jnp.bfloat16)], [core, mine, other], scalars=1
    )[0]
    return whole.reshape(-1, channels)


beta_first = 0.9
beta_second = 0.95
learn_rate = 0.01
decay_rate = 0.1
epsilon = 1e-08

SECTION = ("x_lo", "z")
CHIPS = ("x_hi", "y")


def to_mirror(value):
    length = lax.axis_size(SECTION)
    return lax.ppermute(value, SECTION, [(i, length - 1 - i) for i in range(length)])


def from_next(value):
    length = lax.axis_size(SECTION)
    return lax.ppermute(value, SECTION, [(i + 1, i) for i in range(length - 1)])


def to_partner(value):
    return lax.ppermute(value, "core", [(0, 1), (1, 0)])


def step(acts_down, acts_up, front_down, front_up, master, moment_first, moment_second):
    ticks, _, _, height, width, channels = acts_down.shape
    flat = (height * width, channels)
    chips = lax.axis_size(CHIPS)
    core = lax.axis_index("core").astype(jnp.int32).reshape(1)
    acts_down = [acts_down[t].reshape(flat) for t in range(ticks)]
    acts_up = acts_up.reshape(ticks, *flat)
    mine = lax.all_to_all(spread(master[0], chips), CHIPS, 0, 0, tiled=True)
    front_up = to_mirror(front_up.reshape(flat))
    far_act = to_mirror(acts_up[0])
    far_rest = to_mirror(acts_up[1:])
    hid_down = hidden_parts(acts_down)
    hid_up = hidden_parts([far_act])
    acts_up = [far_act, *far_rest]
    other = to_partner(mine)
    weight = weave(core, mine, other)
    down, up = [front_down.reshape(flat)], [front_up]
    outs_down, outs_up = [], []
    for t in range(ticks):
        next_down = tick(down[t], weight, acts_down[t], width)[0]
        if t + 1 < ticks:
            next_up = tick(up[t], weight, acts_up[t], width)[0]
        else:
            next_up, pair = tick(up[t], weight, acts_up[t], width, outs_up[1])
        outs_down.append(next_down)
        outs_up.append(next_up)
        if t + 1 < ticks:
            down.append(from_next(next_down))
            up.append(from_next(next_up))
    first = to_mirror(outs_up[0])
    hid_up = hid_up + hidden_parts(acts_up[1:])
    total = early_terms([*hid_down[:2], *hid_up[:2]], down[:2] + up[:2], width)
    kept, given = last_terms(core, total, [hid_down[2], hid_up[2]], [down[2], up[2]], chips, width)
    taken = to_partner(given)
    both = pair_add(kept, taken)
    pieces = lax.all_to_all(both, CHIPS, 0, 0, tiled=True)
    pair = to_mirror(pair)
    gradient = jnp.sum(pieces.astype(jnp.float32), axis=0)
    old_master = master[0]
    new_first = beta_first * moment_first[0] + (1.0 - beta_first) * gradient
    new_second = beta_second * moment_second[0] + (1.0 - beta_second) * gradient * gradient
    new_master = old_master - learn_rate * (
        new_first / (jnp.sqrt(new_second) + epsilon) + decay_rate * old_master
    )
    shape = (ticks, 1, 1, height, width, channels)
    return (
        jnp.stack(outs_down).reshape(shape),
        jnp.concatenate([first[None], pair]).reshape(shape),
        new_master.astype(jnp.bfloat16)[None],
        new_master[None],
        new_first[None],
        new_second[None],
    )


def solution(mesh):
    fine = Mesh(
        mesh.devices.reshape(2, 8, 2, 8, 2), ("x_lo", "z", "x_hi", "y", "core")
    )
    dp = (*CHIPS, "core")
    images = P(None, SECTION, dp, None, None, None)
    fronts = P(SECTION, dp, None, None, None)
    rows = P(SECTION, dp, None)
    return jax.shard_map(
        step,
        mesh=fine,
        in_specs=(images, images, fronts, fronts, rows, rows, rows),
        out_specs=(images, images, rows, rows, rows, rows),
        check_vma=False,
    )
```

```python
import functools
import jax
import jax.numpy as jnp
from jax import lax
from jax.experimental import pallas as pl
from jax.experimental.pallas import tpu as pltpu
from jax.sharding import Mesh, PartitionSpec as P


VMEM = pl.BlockSpec(memory_space=pltpu.VMEM)
SMEM = pl.BlockSpec(memory_space=pltpu.SMEM)


def on_chip(value):
    return pltpu.with_memory_space_constraint(value, pltpu.VMEM)


def call(body, outs, args, scratch=(), scalars=0, off_chip=False):
    specs = [SMEM] * scalars + [VMEM] * (len(args) - scalars)
    args = [*args[:scalars], *map(on_chip, args[scalars:])]
    return pl.pallas_call(
        body,
        in_specs=specs,
        out_specs=[VMEM] * len(outs),
        out_shape=[(jax.ShapeDtypeStruct if off_chip else pltpu.VMEM)(*out) for out in outs],
        scratch_shapes=list(scratch),
        compiler_params=pltpu.CompilerParams(vmem_limit_bytes=16 << 20),
    )(*args)


def spread_kernel(rows_ref, out_ref):
    rows = rows_ref[...].astype(jnp.bfloat16)
    for i in range(out_ref.shape[0]):
        out_ref[i] = rows


def spread(rows, count):
    return call(spread_kernel, [((count, *rows.shape), jnp.bfloat16)], [rows])[0]


def add_kernel(one_ref, two_ref, out_ref):
    total = one_ref[...].astype(jnp.float32) + two_ref[...].astype(jnp.float32)
    out_ref[...] = total.astype(jnp.bfloat16)


def pair_add(one, two):
    return call(add_kernel, [(one.shape, jnp.bfloat16)], [one, two])[0]


def bend(x):
    bent = jnp.tanh(0.7978845608028654 * (x + 0.044715 * x * x * x))
    return bent, 0.5 * (1.0 + bent)


def split(pieces):
    arrays = [array for array, _ in pieces]

    def read(refs):
        return [ref[index] for ref, (_, index) in zip(refs, pieces)]

    return arrays, read


def hidden_kernel(read, count, *refs):
    for act, out_ref in zip(read(refs[:count]), refs[count:]):
        x = act.astype(jnp.float32)
        hidden = (x * bend(x)[1]).astype(jnp.bfloat16)
        out_ref[...] = hidden.astype(jnp.float32).T.astype(jnp.bfloat16)


def hidden_parts(acts):
    arrays, read = split(acts)
    outs = [(arrays[0].shape[:0:-1], jnp.bfloat16)] * len(arrays)
    body = functools.partial(hidden_kernel, read, len(arrays))
    return call(body, outs, arrays, off_chip=True)


def keep_kernel(front_ref, out_ref):
    out_ref[...] = front_ref[...]


def keep(front):
    return call(keep_kernel, [(front.shape, front.dtype)], [front])[0]


def fill_taps(front, pad_ref, width):
    pixels = front.shape[0]
    wide = front.astype(jnp.float32)
    column = lax.broadcasted_iota(jnp.int32, wide.shape, 0) % width
    after = jnp.where(column == width - 1, 0.0, pltpu.roll(wide, pixels - 1, 0))
    before = jnp.where(column == 0, 0.0, pltpu.roll(wide, 1, 0))
    empty = jnp.zeros((width, front.shape[1]), jnp.bfloat16)
    for b, piece in enumerate((after.astype(jnp.bfloat16), front, before.astype(jnp.bfloat16))):
        pad_ref[b, 0:width] = empty
        pad_ref[b, width : width + pixels] = piece
        pad_ref[b, width + pixels : 2 * width + pixels] = empty


def pads(count, pixels, width, channels):
    return pltpu.VMEM((count, 3, pixels + 2 * width, channels), jnp.bfloat16)


def tick_kernel(read, width, factor, *refs):
    front_ref, act_ref, weight_ref, *earlier = refs[: len(refs) // 2 + 1]
    out_ref, *pair, pad_ref = refs[len(refs) // 2 + 1 :]
    front, act = read((front_ref, act_ref))
    pixels, channels = front.shape
    fill_taps(front, pad_ref.at[0], width)
    total = jnp.zeros((pixels, channels), jnp.float32)
    for a in range(3):
        for b in range(3):
            row = (3 * a + b) * channels
            total += lax.dot_general(
                pad_ref[0, b, (2 - a) * width : (2 - a) * width + pixels],
                weight_ref[row : row + channels],
                (((1,), (1,)), ((), ())),
                preferred_element_type=jnp.float32,
            )
    x = act.astype(jnp.float32)
    bent, half = bend(x)
    inner = 0.7978845608028654 * (1.0 + 3.0 * 0.044715 * x * x)
    slope = half + 0.5 * x * (1.0 - bent * bent) * inner
    out = (front.astype(jnp.float32) + slope * (factor * total)).astype(jnp.bfloat16)
    out_ref[...] = out
    if pair:
        pair[0][0] = earlier[0][...]
        pair[0][1] = out


def tick(front, act, weight, width, earlier=None):
    arrays, read = split([front, act])
    channels = weight.shape[1]
    pixels = act[0].shape[-2]
    outs = [((pixels, channels), jnp.bfloat16)]
    args = [*arrays, weight]
    if earlier is not None:
        outs.append(((2, pixels, channels), jnp.bfloat16))
        args.append(earlier)
    return call(
        functools.partial(tick_kernel, read, width, (9 * channels) ** -0.5),
        outs,
        args,
        [pads(1, pixels, width, channels)],
    )


def add_terms(hiddens, fronts, pad_ref, width, write):
    for j, front in enumerate(fronts):
        fill_taps(front, pad_ref.at[j], width)
    channels, pixels = hiddens[0].shape
    for a in range(3):
        for b in range(3):
            total = jnp.zeros((channels, channels), jnp.float32)
            for j, hidden in enumerate(hiddens):
                total += lax.dot_general(
                    hidden[...],
                    pad_ref[j, b, (2 - a) * width : (2 - a) * width + pixels],
                    (((1,), (0,)), ((), ())),
                    preferred_element_type=jnp.float32,
                )
            write((3 * a + b) * channels, total)


def early_kernel(read, width, *refs):
    count = len(refs) // 2 - 1
    hid_refs, front_refs, (out_ref, pad_ref) = refs[:count], refs[count:-2], refs[-2:]

    def write(row, total):
        out_ref[row : row + total.shape[0]] = total

    add_terms(hid_refs, read(front_refs), pad_ref, width, write)


def early_terms(hiddens, fronts, width):
    channels, pixels = hiddens[0].shape
    arrays, read = split(fronts)
    return call(
        functools.partial(early_kernel, read, width),
        [((9 * channels, channels), jnp.float32)],
        [*hiddens, *arrays],
        [pads(len(fronts), pixels, width, channels)],
    )[0]


def last_kernel(read, width, factor, core_ref, total_ref, *refs):
    count = len(refs) // 2 - 2
    hid_refs, front_refs = refs[:count], refs[count:-4]
    kept_ref, given_ref, sum_ref, pad_ref = refs[-4:]
    rows = kept_ref.shape[1]

    def write(row, total):
        at = slice(row, row + total.shape[0])
        sum_ref[at] = factor * (total_ref[at] + total)

    add_terms(hid_refs, read(front_refs), pad_ref, width, write)
    for core, places in enumerate(((kept_ref, given_ref), (given_ref, kept_ref))):

        @pl.when(core_ref[0] == core)
        def _():
            for i in range(2 * kept_ref.shape[0]):
                places[i % 2][i // 2] = sum_ref[i * rows : (i + 1) * rows].astype(jnp.bfloat16)


def last_terms(core, total, hiddens, fronts, chips, width):
    channels, pixels = hiddens[0].shape
    half = (chips, 9 * channels // (2 * chips), channels)
    arrays, read = split(fronts)
    return call(
        functools.partial(last_kernel, read, width, (9 * channels) ** -0.5),
        [(half, jnp.bfloat16), (half, jnp.bfloat16)],
        [core, total, *hiddens, *arrays],
        [
            pltpu.VMEM((9 * channels, channels), jnp.float32),
            pads(len(fronts), pixels, width, channels),
        ],
        scalars=1,
    )


def weave_kernel(core_ref, mine_ref, other_ref, out_ref):
    core = core_ref[0]
    for i in range(mine_ref.shape[0]):
        out_ref[i, core] = mine_ref[i]
        out_ref[i, 1 - core] = other_ref[i]


def weave(core, mine, other):
    chips, rows, channels = mine.shape
    whole = call(
        weave_kernel, [((chips, 2, rows, channels), jnp.bfloat16)], [core, mine, other], scalars=1
    )[0]
    return whole.reshape(-1, channels)


beta_first = 0.9
beta_second = 0.95
learn_rate = 0.01
decay_rate = 0.1
epsilon = 1e-08

SECTION = ("x_lo", "z")
CHIPS = ("x_hi", "y")


def to_mirror(value):
    length = lax.axis_size(SECTION)
    return lax.ppermute(value, SECTION, [(i, length - 1 - i) for i in range(length)])


def from_next(value):
    length = lax.axis_size(SECTION)
    return lax.ppermute(value, SECTION, [(i + 1, i) for i in range(length - 1)])


def to_partner(value):
    return lax.ppermute(value, "core", [(0, 1), (1, 0)])


def step(acts_down, acts_up, front_down, front_up, master, moment_first, moment_second):
    ticks, _, _, height, width, channels = acts_down.shape
    flat = (height * width, channels)
    chips = lax.axis_size(CHIPS)
    core = lax.axis_index("core").astype(jnp.int32).reshape(1)
    whole = slice(None)
    acts_down = acts_down.reshape(ticks, *flat)
    acts_up = acts_up.reshape(ticks, *flat)
    mine = lax.all_to_all(spread(master[0], chips), CHIPS, 0, 0, tiled=True)
    far_first = to_mirror(jnp.stack([front_up.reshape(flat), acts_up[0]]))
    far_rest = to_mirror(acts_up[1:])
    front_down = keep(front_down.reshape(flat))
    acts_down = [(acts_down, t) for t in range(ticks)]
    acts_up = [(far_first, 1)] + [(far_rest, t) for t in range(ticks - 1)]
    hid_down = hidden_parts(acts_down)
    other = to_partner(mine)
    weight = weave(core, mine, other)
    down, up = [(front_down, whole)], [(far_first, 0)]
    outs_down, outs_up = [], []
    for t in range(ticks):
        next_down = tick(down[t], acts_down[t], weight, width)[0]
        if t + 1 < ticks:
            next_up = tick(up[t], acts_up[t], weight, width)[0]
        else:
            next_up, pair = tick(up[t], acts_up[t], weight, width, outs_up[1])
        outs_down.append(next_down)
        outs_up.append(next_up)
        if t + 1 < ticks:
            down.append((from_next(next_down), whole))
            up.append((from_next(next_up), whole))
    hid_up = hidden_parts(acts_up)
    total = early_terms([*hid_down[:2], *hid_up[:2]], down[:2] + up[:2], width)
    first = to_mirror(outs_up[0])
    kept, given = last_terms(core, total, [hid_down[2], hid_up[2]], [down[2], up[2]], chips, width)
    taken = to_partner(given)
    both = pair_add(kept, taken)
    pieces = lax.all_to_all(both, CHIPS, 0, 0, tiled=True)
    pair = to_mirror(pair)
    gradient = jnp.sum(pieces.astype(jnp.float32), axis=0)
    old_master = master[0]
    new_first = beta_first * moment_first[0] + (1.0 - beta_first) * gradient
    new_second = beta_second * moment_second[0] + (1.0 - beta_second) * gradient * gradient
    new_master = old_master - learn_rate * (
        new_first / (jnp.sqrt(new_second) + epsilon) + decay_rate * old_master
    )
    shape = (ticks, 1, 1, height, width, channels)
    return (
        jnp.stack(outs_down).reshape(shape),
        jnp.concatenate([first[None], pair]).reshape(shape),
        new_master.astype(jnp.bfloat16)[None],
        new_master[None],
        new_first[None],
        new_second[None],
    )


def solution(mesh):
    fine = Mesh(
        mesh.devices.reshape(2, 8, 2, 8, 2), ("x_lo", "z", "x_hi", "y", "core")
    )
    dp = (*CHIPS, "core")
    images = P(None, SECTION, dp, None, None, None)
    fronts = P(SECTION, dp, None, None, None)
    rows = P(SECTION, dp, None)
    return jax.shard_map(
        step,
        mesh=fine,
        in_specs=(images, images, fronts, fronts, rows, rows, rows),
        out_specs=(images, images, rows, rows, rows, rows),
        check_vma=False,
    )
```

```python
import functools
import jax
import jax.numpy as jnp
from jax import lax
from jax.experimental import pallas as pl
from jax.experimental.pallas import tpu as pltpu
from jax.sharding import Mesh, PartitionSpec as P


VMEM = pl.BlockSpec(memory_space=pltpu.VMEM)
SMEM = pl.BlockSpec(memory_space=pltpu.SMEM)


def on_chip(value):
    return pltpu.with_memory_space_constraint(value, pltpu.VMEM)


def call(body, outs, args, scratch=(), scalars=0, off_chip=False):
    specs = [SMEM] * scalars + [VMEM] * (len(args) - scalars)
    args = [*args[:scalars], *map(on_chip, args[scalars:])]
    return pl.pallas_call(
        body,
        in_specs=specs,
        out_specs=[VMEM] * len(outs),
        out_shape=[(jax.ShapeDtypeStruct if off_chip else pltpu.VMEM)(*out) for out in outs],
        scratch_shapes=list(scratch),
        compiler_params=pltpu.CompilerParams(vmem_limit_bytes=16 << 20),
    )(*args)


def spread_kernel(rows_ref, out_ref):
    rows = rows_ref[...].astype(jnp.bfloat16)
    for i in range(out_ref.shape[0]):
        out_ref[i] = rows


def spread(rows, count):
    steps = 2
    return pl.pallas_call(
        spread_kernel,
        grid=(steps,),
        in_specs=[pl.BlockSpec(rows.shape, lambda i: (0, 0))],
        out_specs=pl.BlockSpec((count // steps, *rows.shape), lambda i: (i, 0, 0)),
        out_shape=jax.ShapeDtypeStruct((count, *rows.shape), jnp.bfloat16),
        name="spread",
    )(rows)


def update_kernel(piece_ref, master_ref, first_ref, second_ref, *outs):
    gradient = piece_ref[0].astype(jnp.float32)
    for i in range(1, piece_ref.shape[0]):
        gradient += piece_ref[i].astype(jnp.float32)
    master = master_ref[...]
    new_first = beta_first * first_ref[...] + (1.0 - beta_first) * gradient
    new_second = beta_second * second_ref[...] + (1.0 - beta_second) * gradient * gradient
    new_master = master - learn_rate * (
        new_first / (jnp.sqrt(new_second) + epsilon) + decay_rate * master
    )
    for out_ref, value in zip(outs, (new_master.astype(jnp.bfloat16), new_master, new_first, new_second)):
        out_ref[...] = value


def update(pieces, master, first, second):
    outs = [(master.shape, jnp.bfloat16)] + [(master.shape, jnp.float32)] * 3
    return call(update_kernel, outs, [pieces, master, first, second], off_chip=True)


def add_kernel(one_ref, two_ref, out_ref):
    total = one_ref[...].astype(jnp.float32) + two_ref[...].astype(jnp.float32)
    out_ref[...] = total.astype(jnp.bfloat16)


def pair_add(one, two):
    return call(add_kernel, [(one.shape, jnp.bfloat16)], [one, two])[0]


def bend(x):
    bent = jnp.tanh(0.7978845608028654 * (x + 0.044715 * x * x * x))
    return bent, 0.5 * (1.0 + bent)


def split(pieces):
    arrays = [array for array, _ in pieces]

    def read(refs):
        return [ref[index] for ref, (_, index) in zip(refs, pieces)]

    return arrays, read


def hidden_kernel(read, count, *refs):
    for act, out_ref in zip(read(refs[:count]), refs[count:]):
        x = act.astype(jnp.float32)
        hidden = (x * bend(x)[1]).astype(jnp.bfloat16)
        out_ref[...] = hidden.astype(jnp.float32).T.astype(jnp.bfloat16)


def hidden_parts(acts):
    arrays, read = split(acts)
    outs = [(arrays[0].shape[:0:-1], jnp.bfloat16)] * len(arrays)
    body = functools.partial(hidden_kernel, read, len(arrays))
    return call(body, outs, arrays, off_chip=True)


def keep_kernel(front_ref, out_ref):
    out_ref[...] = front_ref[...]


def keep(front):
    return call(keep_kernel, [(front.shape, front.dtype)], [front])[0]


def fill_taps(front, pad_ref, width):
    pixels = front.shape[0]
    wide = front.astype(jnp.float32)
    column = lax.broadcasted_iota(jnp.int32, wide.shape, 0) % width
    after = jnp.where(column == width - 1, 0.0, pltpu.roll(wide, pixels - 1, 0))
    before = jnp.where(column == 0, 0.0, pltpu.roll(wide, 1, 0))
    empty = jnp.zeros((width, front.shape[1]), jnp.bfloat16)
    for b, piece in enumerate((after.astype(jnp.bfloat16), front, before.astype(jnp.bfloat16))):
        pad_ref[b, 0:width] = empty
        pad_ref[b, width : width + pixels] = piece
        pad_ref[b, width + pixels : 2 * width + pixels] = empty


def pads(count, pixels, width, channels):
    return pltpu.VMEM((count, 3, pixels + 2 * width, channels), jnp.bfloat16)


def tick_kernel(read, width, factor, *refs):
    front_ref, act_ref, weight_ref, *earlier = refs[: len(refs) // 2 + 1]
    out_ref, *pair, pad_ref = refs[len(refs) // 2 + 1 :]
    front, act = read((front_ref, act_ref))
    pixels, channels = front.shape
    fill_taps(front, pad_ref.at[0], width)
    total = jnp.zeros((pixels, channels), jnp.float32)
    for a in range(3):
        for b in range(3):
            row = (3 * a + b) * channels
            total += lax.dot_general(
                pad_ref[0, b, (2 - a) * width : (2 - a) * width + pixels],
                weight_ref[row : row + channels],
                (((1,), (1,)), ((), ())),
                preferred_element_type=jnp.float32,
            )
    x = act.astype(jnp.float32)
    bent, half = bend(x)
    inner = 0.7978845608028654 * (1.0 + 3.0 * 0.044715 * x * x)
    slope = half + 0.5 * x * (1.0 - bent * bent) * inner
    out = (front.astype(jnp.float32) + slope * (factor * total)).astype(jnp.bfloat16)
    out_ref[...] = out
    if pair:
        pair[0][0] = earlier[0][...]
        pair[0][1] = out


def tick(front, act, weight, width, earlier=None):
    arrays, read = split([front, act])
    channels = weight.shape[1]
    pixels = act[0].shape[-2]
    outs = [((pixels, channels), jnp.bfloat16)]
    args = [*arrays, weight]
    if earlier is not None:
        outs.append(((2, pixels, channels), jnp.bfloat16))
        args.append(earlier)
    return call(
        functools.partial(tick_kernel, read, width, (9 * channels) ** -0.5),
        outs,
        args,
        [pads(1, pixels, width, channels)],
    )


def add_terms(hiddens, fronts, pad_ref, width, write):
    for j, front in enumerate(fronts):
        fill_taps(front, pad_ref.at[j], width)
    channels, pixels = hiddens[0].shape
    for a in range(3):
        for b in range(3):
            total = jnp.zeros((channels, channels), jnp.float32)
            for j, hidden in enumerate(hiddens):
                total += lax.dot_general(
                    hidden[...],
                    pad_ref[j, b, (2 - a) * width : (2 - a) * width + pixels],
                    (((1,), (0,)), ((), ())),
                    preferred_element_type=jnp.float32,
                )
            write((3 * a + b) * channels, total)


def early_kernel(read, width, *refs):
    count = len(refs) // 2 - 1
    hid_refs, front_refs, (out_ref, pad_ref) = refs[:count], refs[count:-2], refs[-2:]

    def write(row, total):
        out_ref[row : row + total.shape[0]] = total

    add_terms(hid_refs, read(front_refs), pad_ref, width, write)


def early_terms(hiddens, fronts, width):
    channels, pixels = hiddens[0].shape
    arrays, read = split(fronts)
    return call(
        functools.partial(early_kernel, read, width),
        [((9 * channels, channels), jnp.float32)],
        [*hiddens, *arrays],
        [pads(len(fronts), pixels, width, channels)],
    )[0]


def last_kernel(read, width, factor, core_ref, total_ref, *refs):
    count = len(refs) // 2 - 2
    hid_refs, front_refs = refs[:count], refs[count:-4]
    kept_ref, given_ref, sum_ref, pad_ref = refs[-4:]
    rows = kept_ref.shape[1]

    def write(row, total):
        at = slice(row, row + total.shape[0])
        sum_ref[at] = factor * (total_ref[at] + total)

    add_terms(hid_refs, read(front_refs), pad_ref, width, write)
    for core, places in enumerate(((kept_ref, given_ref), (given_ref, kept_ref))):

        @pl.when(core_ref[0] == core)
        def _():
            for i in range(2 * kept_ref.shape[0]):
                places[i % 2][i // 2] = sum_ref[i * rows : (i + 1) * rows].astype(jnp.bfloat16)


def last_terms(core, total, hiddens, fronts, chips, width):
    channels, pixels = hiddens[0].shape
    half = (chips, 9 * channels // (2 * chips), channels)
    arrays, read = split(fronts)
    return call(
        functools.partial(last_kernel, read, width, (9 * channels) ** -0.5),
        [(half, jnp.bfloat16), (half, jnp.bfloat16)],
        [core, total, *hiddens, *arrays],
        [
            pltpu.VMEM((9 * channels, channels), jnp.float32),
            pads(len(fronts), pixels, width, channels),
        ],
        scalars=1,
    )


def weave_kernel(core_ref, mine_ref, other_ref, out_ref):
    core = core_ref[0]
    for i in range(mine_ref.shape[0]):
        out_ref[i, core] = mine_ref[i]
        out_ref[i, 1 - core] = other_ref[i]


def weave(core, mine, other):
    chips, rows, channels = mine.shape
    whole = call(
        weave_kernel, [((chips, 2, rows, channels), jnp.bfloat16)], [core, mine, other], scalars=1
    )[0]
    return whole.reshape(-1, channels)


beta_first = 0.9
beta_second = 0.95
learn_rate = 0.01
decay_rate = 0.1
epsilon = 1e-08

SECTION = ("x_lo", "z")
CHIPS = ("x_hi", "y")


def to_mirror(value):
    length = lax.axis_size(SECTION)
    return lax.ppermute(value, SECTION, [(i, length - 1 - i) for i in range(length)])


def from_next(value):
    length = lax.axis_size(SECTION)
    return lax.ppermute(value, SECTION, [(i + 1, i) for i in range(length - 1)])


def to_partner(value):
    return lax.ppermute(value, "core", [(0, 1), (1, 0)])


def step(acts_down, acts_up, front_down, front_up, master, moment_first, moment_second):
    ticks, _, _, height, width, channels = acts_down.shape
    flat = (height * width, channels)
    chips = lax.axis_size(CHIPS)
    core = lax.axis_index("core").astype(jnp.int32).reshape(1)
    whole = slice(None)
    acts_down = acts_down.reshape(ticks, *flat)
    acts_up = acts_up.reshape(ticks, *flat)
    mine = lax.all_to_all(spread(master[0], chips), CHIPS, 0, 0, tiled=True)
    far_first = to_mirror(jnp.stack([front_up.reshape(flat), acts_up[0]]))
    far_rest = to_mirror(acts_up[1:])
    front_down = keep(front_down.reshape(flat))
    acts_down = [(acts_down, t) for t in range(ticks)]
    acts_up = [(far_first, 1)] + [(far_rest, t) for t in range(ticks - 1)]
    hid_down = hidden_parts(acts_down)
    other = to_partner(mine)
    weight = weave(core, mine, other)
    down, up = [(front_down, whole)], [(far_first, 0)]
    outs_down, outs_up = [], []
    for t in range(ticks):
        next_down = tick(down[t], acts_down[t], weight, width)[0]
        if t == 1:
            next_up, pair = tick(up[t], acts_up[t], weight, width, outs_up[0])
        else:
            next_up = tick(up[t], acts_up[t], weight, width)[0]
        outs_down.append(next_down)
        outs_up.append(next_up)
        if t + 1 < ticks:
            down.append((from_next(next_down), whole))
            up.append((from_next(next_up), whole))
    hid_up = hidden_parts(acts_up)
    total = early_terms([*hid_down[:2], *hid_up[:2]], down[:2] + up[:2], width)
    pair = to_mirror(pair)
    kept, given = last_terms(core, total, [hid_down[2], hid_up[2]], [down[2], up[2]], chips, width)
    taken = to_partner(given)
    both = pair_add(kept, taken)
    pieces = lax.all_to_all(both, CHIPS, 0, 0, tiled=True)
    last = to_mirror(outs_up[2])
    new_weight, new_master, new_first, new_second = update(
        pieces, master[0], moment_first[0], moment_second[0]
    )
    shape = (ticks, 1, 1, height, width, channels)
    return (
        jnp.stack(outs_down).reshape(shape),
        jnp.concatenate([pair, last[None]]).reshape(shape),
        new_weight[None],
        new_master[None],
        new_first[None],
        new_second[None],
    )


def solution(mesh):
    fine = Mesh(
        mesh.devices.reshape(2, 8, 2, 8, 2), ("x_lo", "z", "x_hi", "y", "core")
    )
    dp = (*CHIPS, "core")
    images = P(None, SECTION, dp, None, None, None)
    fronts = P(SECTION, dp, None, None, None)
    rows = P(SECTION, dp, None)
    return jax.shard_map(
        step,
        mesh=fine,
        in_specs=(images, images, fronts, fronts, rows, rows, rows),
        out_specs=(images, images, rows, rows, rows, rows),
        check_vma=False,
    )
```

```python
import functools
import jax
import jax.numpy as jnp
from jax import lax
from jax.experimental import pallas as pl
from jax.experimental.pallas import tpu as pltpu
from jax.sharding import Mesh, PartitionSpec as P


VMEM = pl.BlockSpec(memory_space=pltpu.VMEM)
SMEM = pl.BlockSpec(memory_space=pltpu.SMEM)


def on_chip(value):
    return pltpu.with_memory_space_constraint(value, pltpu.VMEM)


def call(body, outs, args, scratch=(), scalars=0, off_chip=False):
    specs = [SMEM] * scalars + [VMEM] * (len(args) - scalars)
    args = [*args[:scalars], *map(on_chip, args[scalars:])]
    return pl.pallas_call(
        body,
        in_specs=specs,
        out_specs=[VMEM] * len(outs),
        out_shape=[(jax.ShapeDtypeStruct if off_chip else pltpu.VMEM)(*out) for out in outs],
        scratch_shapes=list(scratch),
        compiler_params=pltpu.CompilerParams(vmem_limit_bytes=16 << 20),
    )(*args)


def spread_kernel(rows_ref, out_ref, wide_ref, cast_ref, fetch_sem, store_sem):
    fetch = pltpu.make_async_copy(rows_ref, wide_ref, fetch_sem)
    fetch.start()
    fetch.wait()
    cast_ref[...] = wide_ref[...].astype(jnp.bfloat16)
    stores = [
        pltpu.make_async_copy(cast_ref, out_ref.at[i], store_sem.at[i])
        for i in range(out_ref.shape[0])
    ]
    for store in stores:
        store.start()
    for store in stores:
        store.wait()


def spread(rows, count):
    return pl.pallas_call(
        spread_kernel,
        in_specs=[pl.BlockSpec(memory_space=pl.ANY)],
        out_specs=pl.BlockSpec(memory_space=pl.ANY),
        out_shape=jax.ShapeDtypeStruct((count, *rows.shape), jnp.bfloat16),
        scratch_shapes=[
            pltpu.VMEM(rows.shape, jnp.float32),
            pltpu.VMEM(rows.shape, jnp.bfloat16),
            pltpu.SemaphoreType.DMA,
            pltpu.SemaphoreType.DMA((count,)),
        ],
        name="spread",
    )(rows)


def update_kernel(piece_ref, master_ref, first_ref, second_ref, *outs):
    gradient = piece_ref[0].astype(jnp.float32)
    for i in range(1, piece_ref.shape[0]):
        gradient += piece_ref[i].astype(jnp.float32)
    master = master_ref[...]
    new_first = beta_first * first_ref[...] + (1.0 - beta_first) * gradient
    new_second = beta_second * second_ref[...] + (1.0 - beta_second) * gradient * gradient
    new_master = master - learn_rate * (
        new_first / (jnp.sqrt(new_second) + epsilon) + decay_rate * master
    )
    for out_ref, value in zip(outs, (new_master.astype(jnp.bfloat16), new_master, new_first, new_second)):
        out_ref[...] = value


def update(pieces, master, first, second):
    outs = [(master.shape, jnp.bfloat16)] + [(master.shape, jnp.float32)] * 3
    return call(update_kernel, outs, [pieces, master, first, second], off_chip=True)


def add_kernel(one_ref, two_ref, out_ref):
    total = one_ref[...].astype(jnp.float32) + two_ref[...].astype(jnp.float32)
    out_ref[...] = total.astype(jnp.bfloat16)


def pair_add(one, two):
    return call(add_kernel, [(one.shape, jnp.bfloat16)], [one, two])[0]


def bend(x):
    bent = jnp.tanh(0.7978845608028654 * (x + 0.044715 * x * x * x))
    return bent, 0.5 * (1.0 + bent)


def split(pieces):
    arrays = [array for array, _ in pieces]

    def read(refs):
        return [ref[index] for ref, (_, index) in zip(refs, pieces)]

    return arrays, read


def hidden_kernel(read, count, *refs):
    for act, out_ref in zip(read(refs[:count]), refs[count:]):
        x = act.astype(jnp.float32)
        hidden = (x * bend(x)[1]).astype(jnp.bfloat16)
        out_ref[...] = hidden.astype(jnp.float32).T.astype(jnp.bfloat16)


def hidden_parts(acts):
    arrays, read = split(acts)
    outs = [(arrays[0].shape[:0:-1], jnp.bfloat16)] * len(arrays)
    body = functools.partial(hidden_kernel, read, len(arrays))
    return call(body, outs, arrays, off_chip=True)


def keep_kernel(front_ref, out_ref):
    out_ref[...] = front_ref[...]


def keep(front):
    return call(keep_kernel, [(front.shape, front.dtype)], [front])[0]


def fill_taps(front, pad_ref, width):
    pixels = front.shape[0]
    wide = front.astype(jnp.float32)
    column = lax.broadcasted_iota(jnp.int32, wide.shape, 0) % width
    after = jnp.where(column == width - 1, 0.0, pltpu.roll(wide, pixels - 1, 0))
    before = jnp.where(column == 0, 0.0, pltpu.roll(wide, 1, 0))
    empty = jnp.zeros((width, front.shape[1]), jnp.bfloat16)
    for b, piece in enumerate((after.astype(jnp.bfloat16), front, before.astype(jnp.bfloat16))):
        pad_ref[b, 0:width] = empty
        pad_ref[b, width : width + pixels] = piece
        pad_ref[b, width + pixels : 2 * width + pixels] = empty


def pads(count, pixels, width, channels):
    return pltpu.VMEM((count, 3, pixels + 2 * width, channels), jnp.bfloat16)


def tick_kernel(read, width, factor, *refs):
    front_ref, act_ref, weight_ref, *earlier = refs[: len(refs) // 2 + 1]
    out_ref, *pair, pad_ref = refs[len(refs) // 2 + 1 :]
    front, act = read((front_ref, act_ref))
    pixels, channels = front.shape
    fill_taps(front, pad_ref.at[0], width)
    total = jnp.zeros((pixels, channels), jnp.float32)
    for a in range(3):
        for b in range(3):
            row = (3 * a + b) * channels
            total += lax.dot_general(
                pad_ref[0, b, (2 - a) * width : (2 - a) * width + pixels],
                weight_ref[row : row + channels],
                (((1,), (1,)), ((), ())),
                preferred_element_type=jnp.float32,
            )
    x = act.astype(jnp.float32)
    bent, half = bend(x)
    inner = 0.7978845608028654 * (1.0 + 3.0 * 0.044715 * x * x)
    slope = half + 0.5 * x * (1.0 - bent * bent) * inner
    out = (front.astype(jnp.float32) + slope * (factor * total)).astype(jnp.bfloat16)
    out_ref[...] = out
    if pair:
        pair[0][0] = earlier[0][...]
        pair[0][1] = out


def tick(front, act, weight, width, earlier=None):
    arrays, read = split([front, act])
    channels = weight.shape[1]
    pixels = act[0].shape[-2]
    outs = [((pixels, channels), jnp.bfloat16)]
    args = [*arrays, weight]
    if earlier is not None:
        outs.append(((2, pixels, channels), jnp.bfloat16))
        args.append(earlier)
    return call(
        functools.partial(tick_kernel, read, width, (9 * channels) ** -0.5),
        outs,
        args,
        [pads(1, pixels, width, channels)],
    )


def add_terms(hiddens, fronts, pad_ref, width, write):
    for j, front in enumerate(fronts):
        fill_taps(front, pad_ref.at[j], width)
    channels, pixels = hiddens[0].shape
    for a in range(3):
        for b in range(3):
            total = jnp.zeros((channels, channels), jnp.float32)
            for j, hidden in enumerate(hiddens):
                total += lax.dot_general(
                    hidden[...],
                    pad_ref[j, b, (2 - a) * width : (2 - a) * width + pixels],
                    (((1,), (0,)), ((), ())),
                    preferred_element_type=jnp.float32,
                )
            write((3 * a + b) * channels, total)


def early_kernel(read, width, *refs):
    count = len(refs) // 2 - 1
    hid_refs, front_refs, (out_ref, pad_ref) = refs[:count], refs[count:-2], refs[-2:]

    def write(row, total):
        out_ref[row : row + total.shape[0]] = total

    add_terms(hid_refs, read(front_refs), pad_ref, width, write)


def early_terms(hiddens, fronts, width):
    channels, pixels = hiddens[0].shape
    arrays, read = split(fronts)
    return call(
        functools.partial(early_kernel, read, width),
        [((9 * channels, channels), jnp.float32)],
        [*hiddens, *arrays],
        [pads(len(fronts), pixels, width, channels)],
    )[0]


def last_kernel(read, width, factor, core_ref, total_ref, *refs):
    count = len(refs) // 2 - 2
    hid_refs, front_refs = refs[:count], refs[count:-4]
    kept_ref, given_ref, sum_ref, pad_ref = refs[-4:]
    rows = kept_ref.shape[1]

    def write(row, total):
        at = slice(row, row + total.shape[0])
        sum_ref[at] = factor * (total_ref[at] + total)

    add_terms(hid_refs, read(front_refs), pad_ref, width, write)
    for core, places in enumerate(((kept_ref, given_ref), (given_ref, kept_ref))):

        @pl.when(core_ref[0] == core)
        def _():
            for i in range(2 * kept_ref.shape[0]):
                places[i % 2][i // 2] = sum_ref[i * rows : (i + 1) * rows].astype(jnp.bfloat16)


def last_terms(core, total, hiddens, fronts, chips, width):
    channels, pixels = hiddens[0].shape
    half = (chips, 9 * channels // (2 * chips), channels)
    arrays, read = split(fronts)
    return call(
        functools.partial(last_kernel, read, width, (9 * channels) ** -0.5),
        [(half, jnp.bfloat16), (half, jnp.bfloat16)],
        [core, total, *hiddens, *arrays],
        [
            pltpu.VMEM((9 * channels, channels), jnp.float32),
            pads(len(fronts), pixels, width, channels),
        ],
        scalars=1,
    )


def weave_kernel(core_ref, mine_ref, other_ref, out_ref):
    core = core_ref[0]
    for i in range(mine_ref.shape[0]):
        out_ref[i, core] = mine_ref[i]
        out_ref[i, 1 - core] = other_ref[i]


def weave(core, mine, other):
    chips, rows, channels = mine.shape
    whole = call(
        weave_kernel, [((chips, 2, rows, channels), jnp.bfloat16)], [core, mine, other], scalars=1
    )[0]
    return whole.reshape(-1, channels)


beta_first = 0.9
beta_second = 0.95
learn_rate = 0.01
decay_rate = 0.1
epsilon = 1e-08

SECTION = ("x_lo", "z")
CHIPS = ("x_hi", "y")


def to_mirror(value):
    length = lax.axis_size(SECTION)
    return lax.ppermute(value, SECTION, [(i, length - 1 - i) for i in range(length)])


def from_next(value):
    length = lax.axis_size(SECTION)
    return lax.ppermute(value, SECTION, [(i + 1, i) for i in range(length - 1)])


def to_partner(value):
    return lax.ppermute(value, "core", [(0, 1), (1, 0)])


def step(acts_down, acts_up, front_down, front_up, master, moment_first, moment_second):
    ticks, _, _, height, width, channels = acts_down.shape
    flat = (height * width, channels)
    chips = lax.axis_size(CHIPS)
    core = lax.axis_index("core").astype(jnp.int32).reshape(1)
    whole = slice(None)
    acts_down = acts_down.reshape(ticks, *flat)
    acts_up = acts_up.reshape(ticks, *flat)
    mine = lax.all_to_all(spread(master[0], chips), CHIPS, 0, 0, tiled=True)
    front_up = to_mirror(front_up.reshape(flat))
    acts_up = to_mirror(acts_up)
    front_down = keep(front_down.reshape(flat))
    acts_down = [(acts_down, t) for t in range(ticks)]
    acts_up = [(acts_up, t) for t in range(ticks)]
    hid_down = hidden_parts(acts_down)
    other = to_partner(mine)
    weight = weave(core, mine, other)
    down, up = [(front_down, whole)], [(front_up, whole)]
    outs_down, outs_up = [], []
    for t in range(ticks):
        next_down = tick(down[t], acts_down[t], weight, width)[0]
        if t == 1:
            next_up, pair = tick(up[t], acts_up[t], weight, width, outs_up[0])
        else:
            next_up = tick(up[t], acts_up[t], weight, width)[0]
        outs_down.append(next_down)
        outs_up.append(next_up)
        if t + 1 < ticks:
            down.append((from_next(next_down), whole))
            up.append((from_next(next_up), whole))
    hid_up = hidden_parts(acts_up)
    total = early_terms([*hid_down[:2], *hid_up[:2]], down[:2] + up[:2], width)
    pair = to_mirror(pair)
    kept, given = last_terms(core, total, [hid_down[2], hid_up[2]], [down[2], up[2]], chips, width)
    taken = to_partner(given)
    both = pair_add(kept, taken)
    pieces = lax.all_to_all(both, CHIPS, 0, 0, tiled=True)
    last = to_mirror(outs_up[2])
    new_weight, new_master, new_first, new_second = update(
        pieces, master[0], moment_first[0], moment_second[0]
    )
    shape = (ticks, 1, 1, height, width, channels)
    return (
        jnp.stack(outs_down).reshape(shape),
        jnp.concatenate([pair, last[None]]).reshape(shape),
        new_weight[None],
        new_master[None],
        new_first[None],
        new_second[None],
    )


def solution(mesh):
    fine = Mesh(
        mesh.devices.reshape(2, 8, 2, 8, 2), ("x_lo", "z", "x_hi", "y", "core")
    )
    dp = (*CHIPS, "core")
    images = P(None, SECTION, dp, None, None, None)
    fronts = P(SECTION, dp, None, None, None)
    rows = P(SECTION, dp, None)
    return jax.shard_map(
        step,
        mesh=fine,
        in_specs=(images, images, fronts, fronts, rows, rows, rows),
        out_specs=(images, images, rows, rows, rows, rows),
        check_vma=False,
    )
```

```python
import functools
import jax
import jax.numpy as jnp
from jax import lax
from jax.experimental import pallas as pl
from jax.experimental.pallas import tpu as pltpu
from jax.sharding import Mesh, PartitionSpec as P


VMEM = pl.BlockSpec(memory_space=pltpu.VMEM)
SMEM = pl.BlockSpec(memory_space=pltpu.SMEM)


def on_chip(value):
    return pltpu.with_memory_space_constraint(value, pltpu.VMEM)


def call(body, outs, args, scratch=(), scalars=0, off_chip=False):
    specs = [SMEM] * scalars + [VMEM] * (len(args) - scalars)
    args = [*args[:scalars], *map(on_chip, args[scalars:])]
    return pl.pallas_call(
        body,
        in_specs=specs,
        out_specs=[VMEM] * len(outs),
        out_shape=[(jax.ShapeDtypeStruct if off_chip else pltpu.VMEM)(*out) for out in outs],
        scratch_shapes=list(scratch),
        compiler_params=pltpu.CompilerParams(vmem_limit_bytes=16 << 20),
    )(*args)


def send_out(cast_ref, out_ref, sem, places):
    return [
        pltpu.make_async_copy(cast_ref.at[at], out_ref.at[to], sem.at[i])
        for i, (at, to) in enumerate(places)
    ]


def spread_kernel(rows_ref, out_ref, cast_ref, sem):
    cast_ref[...] = rows_ref[...].astype(jnp.bfloat16)
    stores = send_out(cast_ref, out_ref, sem, [(slice(None), i) for i in range(out_ref.shape[0])])
    for store in stores:
        store.start()
    for store in stores:
        store.wait()


def spread(rows, count):
    return pl.pallas_call(
        spread_kernel,
        in_specs=[VMEM],
        out_specs=pl.BlockSpec(memory_space=pl.ANY),
        out_shape=jax.ShapeDtypeStruct((count, *rows.shape), jnp.bfloat16),
        scratch_shapes=[
            pltpu.VMEM(rows.shape, jnp.bfloat16),
            pltpu.SemaphoreType.DMA((count,)),
        ],
        name="spread",
        compiler_params=pltpu.CompilerParams(vmem_limit_bytes=16 << 20),
    )(on_chip(rows))


def update_kernel(piece_ref, master_ref, first_ref, second_ref, *outs):
    gradient = piece_ref[0].astype(jnp.float32)
    for i in range(1, piece_ref.shape[0]):
        gradient += piece_ref[i].astype(jnp.float32)
    master = master_ref[...]
    new_first = beta_first * first_ref[...] + (1.0 - beta_first) * gradient
    new_second = beta_second * second_ref[...] + (1.0 - beta_second) * gradient * gradient
    new_master = master - learn_rate * (
        new_first / (jnp.sqrt(new_second) + epsilon) + decay_rate * master
    )
    for out_ref, value in zip(outs, (new_master.astype(jnp.bfloat16), new_master, new_first, new_second)):
        out_ref[...] = value


def update(pieces, master, first, second):
    outs = [(master.shape, jnp.bfloat16)] + [(master.shape, jnp.float32)] * 3
    return call(update_kernel, outs, [pieces, master, first, second], off_chip=True)


def add_kernel(one_ref, two_ref, out_ref, cast_ref, sem):
    chips = one_ref.shape[0]
    step = chips // sem.shape[0]
    places = [(slice(i, i + step), slice(i, i + step)) for i in range(0, chips, step)]
    stores = send_out(cast_ref, out_ref, sem, places)
    for store, (at, _) in zip(stores, places):
        total = one_ref[at].astype(jnp.float32) + two_ref[at].astype(jnp.float32)
        cast_ref[at] = total.astype(jnp.bfloat16)
        store.start()
    for store in stores:
        store.wait()


def pair_add(one, two):
    return pl.pallas_call(
        add_kernel,
        in_specs=[VMEM] * 2,
        out_specs=pl.BlockSpec(memory_space=pl.ANY),
        out_shape=jax.ShapeDtypeStruct(one.shape, jnp.bfloat16),
        scratch_shapes=[pltpu.VMEM(one.shape, jnp.bfloat16), pltpu.SemaphoreType.DMA((4,))],
        name="pair_add",
        compiler_params=pltpu.CompilerParams(vmem_limit_bytes=16 << 20),
    )(on_chip(one), on_chip(two))


def bend(x):
    bent = jnp.tanh(0.7978845608028654 * (x + 0.044715 * x * x * x))
    return bent, 0.5 * (1.0 + bent)


def split(pieces):
    arrays = [array for array, _ in pieces]

    def read(refs):
        return [ref[index] for ref, (_, index) in zip(refs, pieces)]

    return arrays, read


def hidden_kernel(read, count, *refs):
    for act, out_ref in zip(read(refs[:count]), refs[count:]):
        x = act.astype(jnp.float32)
        hidden = (x * bend(x)[1]).astype(jnp.bfloat16)
        out_ref[...] = hidden.astype(jnp.float32).T.astype(jnp.bfloat16)


def hidden_parts(acts):
    arrays, read = split(acts)
    outs = [(arrays[0].shape[:0:-1], jnp.bfloat16)] * len(arrays)
    body = functools.partial(hidden_kernel, read, len(arrays))
    return call(body, outs, arrays, off_chip=True)


def keep_kernel(front_ref, out_ref):
    out_ref[...] = front_ref[...]


def keep(front):
    return call(keep_kernel, [(front.shape, front.dtype)], [front])[0]


def fill_taps(front, pad_ref, width):
    pixels = front.shape[0]
    wide = front.astype(jnp.float32)
    column = lax.broadcasted_iota(jnp.int32, wide.shape, 0) % width
    after = jnp.where(column == width - 1, 0.0, pltpu.roll(wide, pixels - 1, 0))
    before = jnp.where(column == 0, 0.0, pltpu.roll(wide, 1, 0))
    empty = jnp.zeros((width, front.shape[1]), jnp.bfloat16)
    for b, piece in enumerate((after.astype(jnp.bfloat16), front, before.astype(jnp.bfloat16))):
        pad_ref[b, 0:width] = empty
        pad_ref[b, width : width + pixels] = piece
        pad_ref[b, width + pixels : 2 * width + pixels] = empty


def pads(count, pixels, width, channels):
    return pltpu.VMEM((count, 3, pixels + 2 * width, channels), jnp.bfloat16)


def tick_kernel(read, width, factor, *refs):
    front_ref, act_ref, weight_ref, *earlier = refs[: len(refs) // 2 + 1]
    out_ref, *pair, pad_ref = refs[len(refs) // 2 + 1 :]
    front, act = read((front_ref, act_ref))
    pixels, channels = front.shape
    fill_taps(front, pad_ref.at[0], width)
    total = jnp.zeros((pixels, channels), jnp.float32)
    for a in range(3):
        for b in range(3):
            row = (3 * a + b) * channels
            total += lax.dot_general(
                pad_ref[0, b, (2 - a) * width : (2 - a) * width + pixels],
                weight_ref[row : row + channels],
                (((1,), (1,)), ((), ())),
                preferred_element_type=jnp.float32,
            )
    x = act.astype(jnp.float32)
    bent, half = bend(x)
    inner = 0.7978845608028654 * (1.0 + 3.0 * 0.044715 * x * x)
    slope = half + 0.5 * x * (1.0 - bent * bent) * inner
    out = (front.astype(jnp.float32) + slope * (factor * total)).astype(jnp.bfloat16)
    out_ref[...] = out
    if pair:
        pair[0][0] = earlier[0][...]
        pair[0][1] = out


def tick(front, act, weight, width, earlier=None):
    arrays, read = split([front, act])
    channels = weight.shape[1]
    pixels = act[0].shape[-2]
    outs = [((pixels, channels), jnp.bfloat16)]
    args = [*arrays, weight]
    if earlier is not None:
        outs.append(((2, pixels, channels), jnp.bfloat16))
        args.append(earlier)
    return call(
        functools.partial(tick_kernel, read, width, (9 * channels) ** -0.5),
        outs,
        args,
        [pads(1, pixels, width, channels)],
    )


def add_terms(hiddens, fronts, pad_ref, width, write):
    for j, front in enumerate(fronts):
        fill_taps(front, pad_ref.at[j], width)
    channels, pixels = hiddens[0].shape
    for a in range(3):
        for b in range(3):
            total = jnp.zeros((channels, channels), jnp.float32)
            for j, hidden in enumerate(hiddens):
                total += lax.dot_general(
                    hidden[...],
                    pad_ref[j, b, (2 - a) * width : (2 - a) * width + pixels],
                    (((1,), (0,)), ((), ())),
                    preferred_element_type=jnp.float32,
                )
            write((3 * a + b) * channels, total)


def early_kernel(read, width, *refs):
    count = len(refs) // 2 - 1
    hid_refs, front_refs, (out_ref, pad_ref) = refs[:count], refs[count:-2], refs[-2:]

    def write(row, total):
        out_ref[row : row + total.shape[0]] = total

    add_terms(hid_refs, read(front_refs), pad_ref, width, write)


def early_terms(hiddens, fronts, width):
    channels, pixels = hiddens[0].shape
    arrays, read = split(fronts)
    return call(
        functools.partial(early_kernel, read, width),
        [((9 * channels, channels), jnp.float32)],
        [*hiddens, *arrays],
        [pads(len(fronts), pixels, width, channels)],
    )[0]


def last_kernel(read, width, factor, core_ref, total_ref, *refs):
    count = len(refs) // 2 - 2
    hid_refs, front_refs = refs[:count], refs[count:-4]
    kept_ref, given_ref, sum_ref, pad_ref = refs[-4:]
    rows = kept_ref.shape[1]

    def write(row, total):
        at = slice(row, row + total.shape[0])
        sum_ref[at] = factor * (total_ref[at] + total)

    add_terms(hid_refs, read(front_refs), pad_ref, width, write)
    for core, places in enumerate(((kept_ref, given_ref), (given_ref, kept_ref))):

        @pl.when(core_ref[0] == core)
        def _():
            for i in range(2 * kept_ref.shape[0]):
                places[i % 2][i // 2] = sum_ref[i * rows : (i + 1) * rows].astype(jnp.bfloat16)


def last_terms(core, total, hiddens, fronts, chips, width):
    channels, pixels = hiddens[0].shape
    half = (chips, 9 * channels // (2 * chips), channels)
    arrays, read = split(fronts)
    return call(
        functools.partial(last_kernel, read, width, (9 * channels) ** -0.5),
        [(half, jnp.bfloat16), (half, jnp.bfloat16)],
        [core, total, *hiddens, *arrays],
        [
            pltpu.VMEM((9 * channels, channels), jnp.float32),
            pads(len(fronts), pixels, width, channels),
        ],
        scalars=1,
    )


def weave_kernel(core_ref, mine_ref, other_ref, out_ref):
    core = core_ref[0]
    for i in range(mine_ref.shape[0]):
        out_ref[i, core] = mine_ref[i]
        out_ref[i, 1 - core] = other_ref[i]


def weave(core, mine, other):
    chips, rows, channels = mine.shape
    whole = call(
        weave_kernel, [((chips, 2, rows, channels), jnp.bfloat16)], [core, mine, other], scalars=1
    )[0]
    return whole.reshape(-1, channels)


beta_first = 0.9
beta_second = 0.95
learn_rate = 0.01
decay_rate = 0.1
epsilon = 1e-08

SECTION = ("x_lo", "z")
CHIPS = ("x_hi", "y")


def to_mirror(value):
    length = lax.axis_size(SECTION)
    return lax.ppermute(value, SECTION, [(i, length - 1 - i) for i in range(length)])


def from_next(value):
    length = lax.axis_size(SECTION)
    return lax.ppermute(value, SECTION, [(i + 1, i) for i in range(length - 1)])


def to_partner(value):
    return lax.ppermute(value, "core", [(0, 1), (1, 0)])


def step(acts_down, acts_up, front_down, front_up, master, moment_first, moment_second):
    ticks, _, _, height, width, channels = acts_down.shape
    flat = (height * width, channels)
    chips = lax.axis_size(CHIPS)
    core = lax.axis_index("core").astype(jnp.int32).reshape(1)
    whole = slice(None)
    acts_down = acts_down.reshape(ticks, *flat)
    acts_up = acts_up.reshape(ticks, *flat)
    mine = lax.all_to_all(spread(master[0], chips), CHIPS, 0, 0, tiled=True)
    front_up = to_mirror(front_up.reshape(flat))
    acts_up = to_mirror(acts_up)
    front_down = keep(front_down.reshape(flat))
    acts_down = [(acts_down, t) for t in range(ticks)]
    acts_up = [(acts_up, t) for t in range(ticks)]
    hid_down = hidden_parts(acts_down)
    other = to_partner(mine)
    weight = weave(core, mine, other)
    down, up = [(front_down, whole)], [(front_up, whole)]
    outs_down, outs_up = [], []
    for t in range(ticks):
        next_down = tick(down[t], acts_down[t], weight, width)[0]
        if t == 1:
            next_up, pair = tick(up[t], acts_up[t], weight, width, outs_up[0])
        else:
            next_up = tick(up[t], acts_up[t], weight, width)[0]
        outs_down.append(next_down)
        outs_up.append(next_up)
        if t + 1 < ticks:
            down.append((from_next(next_down), whole))
            up.append((from_next(next_up), whole))
    hid_up = hidden_parts(acts_up)
    total = early_terms([*hid_down[:2], *hid_up[:2]], down[:2] + up[:2], width)
    pair = to_mirror(pair)
    kept, given = last_terms(core, total, [hid_down[2], hid_up[2]], [down[2], up[2]], chips, width)
    taken = to_partner(given)
    both = pair_add(kept, taken)
    pieces = lax.all_to_all(both, CHIPS, 0, 0, tiled=True)
    last = to_mirror(outs_up[2])
    new_weight, new_master, new_first, new_second = update(
        pieces, master[0], moment_first[0], moment_second[0]
    )
    shape = (ticks, 1, 1, height, width, channels)
    return (
        jnp.stack(outs_down).reshape(shape),
        jnp.concatenate([pair, last[None]]).reshape(shape),
        new_weight[None],
        new_master[None],
        new_first[None],
        new_second[None],
    )


def solution(mesh):
    fine = Mesh(
        mesh.devices.reshape(2, 8, 2, 8, 2), ("x_lo", "z", "x_hi", "y", "core")
    )
    dp = (*CHIPS, "core")
    images = P(None, SECTION, dp, None, None, None)
    fronts = P(SECTION, dp, None, None, None)
    rows = P(SECTION, dp, None)
    return jax.shard_map(
        step,
        mesh=fine,
        in_specs=(images, images, fronts, fronts, rows, rows, rows),
        out_specs=(images, images, rows, rows, rows, rows),
        check_vma=False,
    )
```
